256 devices in a mesh: feat: 32 (over x_lo, z, core), tok: 8 (over x_hi, y).
Axes of the slice: x: 4 (x_hi: 2, x_lo: 2; x = x_hi * 2 + x_lo), y: 4, z: 8, core: 2. Of those that a mesh axis runs over, the one named last changes fastest.
Arguments:
- acts_in: bfloat16 [3072, 2, 2304], P(('tok', 'feat')), may hold values from -6 to 6
- targets: bfloat16 [3072, 2, 2304], P(('tok', 'feat')), may hold values from -6 to 6
- enc_weight: bfloat16 [2, 2304, 16384], P(None, None, 'feat'), may hold values from -0.125 to 0.125
- enc_bias: float32 [2, 16384], P(None, 'feat'), may hold values from -3 to 3
- dec_weight: bfloat16 [3, 16384, 2304], P(None, 'feat'), may hold values from -0.046875 to 0.046875
Outputs:
- grad_enc: bfloat16 [2, 2304, 16384], P(None, 'tok', 'feat')
- grad_enc_bias: float32 [2, 16384], P(None, ('feat', 'tok'))
- grad_dec: bfloat16 [3, 16384, 2304], P(None, ('feat', 'tok'))
The draws below stay inside these ranges and needn't reach their ends.
All inputs are finite; a program needn't handle non-finite values.
Results may differ from the reference program's by a relative error of at most 0.02.
Values may be sent and summed in bfloat16 or wider, within the bound.
A program may use at most 128 MiB of HBM per device.

```python
import math
import jax
import jax.numpy as jnp
from jax import lax

D = 2304
F = 16384
L = 2
TOK_DEV = 384
PAIRS = 3
TOKENS = 3072


def level_of(key, extent, shards, smallest, high):
    def one(dim, blocks):
        draws = jax.random.uniform(jax.random.fold_in(jax.random.fold_in(key, 6), dim), (blocks,), jnp.float32, smallest / len(shards), high / len(shards))
        return jnp.repeat(jnp.exp(draws), extent[dim] // blocks).reshape((-1,) + (1,) * (len(extent) - dim - 1))

    level = one(*shards[0])
    for cut in shards[1:]:
        level = level * one(*cut)
    return level


def centred(stream_key, extent, scale, most, split=(), kind=jnp.bfloat16):
    loudness = level_of(stream_key, extent, split, -0.22, 0.18) if split else 1.0
    result = jax.random.normal(stream_key, extent, jnp.float32) * scale * loudness
    return jnp.minimum(jnp.maximum(result, -most), most).astype(kind)


def setup_inputs(seed: int = 0) -> dict:
    keys = jax.random.split(jax.random.key(seed), 6)
    acts_in = centred(keys[0], (TOKENS, L, D), 1.0, 6.0, ((0, 256),))
    targets = centred(keys[1], (TOKENS, L, D), 1.0, 6.0, ((0, 256),))
    enc_weight = centred(keys[2], (L, D, F), D ** -0.5, 0.125, ((2, 32),))
    enc_bias = centred(keys[3], (L, F), 0.5, 3.0, ((1, 32),), jnp.float32)
    dec_weight = centred(keys[4], (PAIRS, F, D), F ** -0.5, 0.046875, ((1, 32),))
    return {"acts_in": acts_in, "targets": targets, "enc_weight": enc_weight, "enc_bias": enc_bias, "dec_weight": dec_weight}


def pair_slot(source, target, layers):
    return sum((layers - k for k in range(source))) + (target - source)

def reference(acts_in, targets, enc_weight, enc_bias, dec_weight):
    layers = L
    preacts = []
    coded = []
    for source in range(layers):
        value = jnp.dot(acts_in[:, source, :], enc_weight[source], preferred_element_type=jnp.float32) + enc_bias[source]
        preacts.append(value)
        coded.append((0.5 * jnp.maximum(value, 0.0) ** 2).astype(jnp.bfloat16))
    rebuilt = []
    for target in range(layers):
        total = jnp.zeros((acts_in.shape[0], D), jnp.float32)
        for source in range(target + 1):
            total = total + jnp.dot(coded[source], dec_weight[pair_slot(source, target, layers)], preferred_element_type=jnp.float32)
        rebuilt.append(total)
    errors = (jnp.stack(rebuilt, axis=1) - targets.astype(jnp.float32)).astype(jnp.bfloat16)
    dpreacts = []
    for source in range(layers):
        dcoded = jnp.zeros((acts_in.shape[0], F), jnp.float32)
        for target in range(source, layers):
            dcoded = dcoded + lax.dot_general(errors[:, target, :], dec_weight[pair_slot(source, target, layers)], (((1,), (1,)), ((), ())), preferred_element_type=jnp.float32)
        dpreacts.append((dcoded * jnp.maximum(preacts[source], 0.0)).astype(jnp.bfloat16))
    loss_scale = 1.0 / math.sqrt(TOKENS)
    groups = TOKENS // TOK_DEV
    inputs_g = acts_in.reshape(groups, TOK_DEV, layers, D)
    errors_g = errors.reshape(groups, TOK_DEV, layers, D)
    coded_g = jnp.stack(coded, axis=0).reshape(layers, groups, TOK_DEV, F).transpose(1, 0, 2, 3)
    dpre_g = jnp.stack(dpreacts, axis=0).reshape(layers, groups, TOK_DEV, F).transpose(1, 0, 2, 3)

    def step(carry, group):
        enc_sum, bias_sum, dec_sum = carry
        inputs, errs, codes, dpres = group
        enc_parts = []
        bias_parts = []
        for source in range(layers):
            part = jnp.dot(inputs[:, source, :].T, dpres[source], preferred_element_type=jnp.float32) * loss_scale
            enc_parts.append(part.astype(jnp.bfloat16).astype(jnp.float32))
            bias_part = lax.optimization_barrier(jnp.sum(dpres[source].astype(jnp.float32), axis=0)) * loss_scale
            bias_parts.append(bias_part.astype(jnp.bfloat16).astype(jnp.float32))
        dec_parts = []
        for source in range(layers):
            for target in range(source, layers):
                part = jnp.dot(codes[source].T, errs[:, target, :], preferred_element_type=jnp.float32) * loss_scale
                dec_parts.append(part.astype(jnp.bfloat16).astype(jnp.float32))
        return ((enc_sum + jnp.stack(enc_parts), bias_sum + jnp.stack(bias_parts), dec_sum + jnp.stack(dec_parts)), None)
    start = (jnp.zeros((layers, D, F), jnp.float32), jnp.zeros((layers, F), jnp.float32), jnp.zeros((PAIRS, F, D), jnp.float32))
    (enc_sum, bias_sum, dec_sum), _ = lax.scan(step, start, (inputs_g, errors_g, coded_g, dpre_g))
    return (enc_sum.astype(jnp.bfloat16), bias_sum, dec_sum.astype(jnp.bfloat16))
```

```python
import math

import jax
import jax.numpy as jnp
from jax import lax
from jax.experimental import pallas as pl
from jax.experimental.pallas import tpu as pltpu
from jax.sharding import PartitionSpec as P

MESH = pl.DeviceIdType.MESH
F32 = jnp.float32
BF16 = jnp.bfloat16
XN, ZN, YN = 4, 8, 4
TD = 12
ROWS = XN * TD
COLS = 1152
FH = 256
AG_ORDER = (0, -1, 1, -2, 2, -3, 3, 4)
RS_ORDER = (4, 3, -3, 2, -2, 1, -1, 0)
PAIR = {(0, 0): 0, (0, 1): 1, (1, 1): 2}


def kernel(inp, eb, ew_hbm, dw_hbm, ge_out, gb_out, gd_out,
           land, acts, tgt, errs, ew, dw, gate, coded, coded_t, dpre, part, sib, recv,
           gdec, genc, rone_d, rone_e, rtwo_d, rtwo_e, swap, bsum, bland,
           wsem, a2a_s, a2a_r, ag1_s, ag1_r, rs_s, rs_r, ag2_s, ag2_r, y_s, y_r, b_s, b_r, sw_s, sw_r):
    fi = lax.axis_index("feat")
    ti = lax.axis_index("tok")
    core = fi % 2
    z = (fi // 2) % ZN
    xlo = fi // (2 * ZN)
    y = ti % YN
    xhi = ti // YN
    x = 2 * xhi + xlo
    scale = 1.0 / math.sqrt(3072.0)

    def dev(xx, zz, yy, cc):
        return ((xx % 2) * (2 * ZN) + zz * 2 + cc, (xx // 2) * YN + yy)

    def xd(d):
        return dev((x + d) % XN, z, y, core)

    def zd(d):
        return dev(x, (z + d + ZN) % ZN, y, core)

    def yd(d):
        return dev(x, z, (y + d) % YN, core)

    def zat(s):
        return (z + s + ZN) % ZN

    def xat(d):
        return (x + d) % XN

    sibling = dev(x, z, y, 1 - core)

    def rcopy(src, dst, ssem, rsem, device):
        return pltpu.make_async_remote_copy(src_ref=src, dst_ref=dst, send_sem=ssem, recv_sem=rsem, device_id=device, device_id_type=MESH)

    def got(dst, rsem):
        rcopy(dst, dst, rsem, rsem, sibling).wait_recv()

    fo = pl.multiple_of(xhi * FH, FH)
    w_copies = [pltpu.make_async_copy(ew_hbm.at[:, :, pl.ds(fo, FH)], ew, wsem.at[0]),
                pltpu.make_async_copy(dw_hbm.at[:, pl.ds(fo, FH), :], dw, wsem.at[1])]
    for copy in w_copies:
        copy.start()

    barrier = pltpu.get_barrier_semaphore()
    partners = [sibling] + [xd(d) for d in (1, 2, 3)] + [zd(1), zd(-1)] + [yd(d) for d in (1, 2, 3)]
    for partner in partners:
        pl.semaphore_signal(barrier, inc=1, device_id=partner, device_id_type=MESH)
    pl.semaphore_wait(barrier, len(partners))

    sends = []
    for d in (1, 2, 3):
        send = rcopy(inp.at[:, xat(d)], land.at[:, d], a2a_s.at[d], a2a_r.at[d], xd(d))
        send.start()
        sends.append(send)
    land[:, 0] = inp[:, x]
    row = lax.broadcasted_iota(jnp.int32, (ROWS, XN * 16), 0)
    col = lax.broadcasted_iota(jnp.int32, (ROWS, XN * 16), 1)
    source = (x + XN - col // 16) % XN
    place = jnp.where((row == TD * source + col % 16) & (col % 16 < TD), 1.0, 0.0).astype(BF16)
    for d in (1, 2, 3):
        got(land.at[:, d], a2a_r.at[d])
    acts[x, z, core] = jnp.dot(place, land[0].reshape(XN * 16, COLS), preferred_element_type=F32).astype(BF16)
    tgt[...] = jnp.dot(place, land[1].reshape(XN * 16, COLS), preferred_element_type=F32)

    def gather(buf, s_sem, r_sem):
        @pl.when(core == 0)
        def _():
            out = []

            def send(xx, zz, device, r):
                unit = buf.at[xx, zz, 0]
                one = rcopy(unit, unit, s_sem.at[len(out)], r_sem.at[r], device)
                one.start()
                out.append(one)

            def to_x(i):
                zz = zat(AG_ORDER[i])
                send(x, zz, xd(1), 8 + i)
                send(x, zz, xd(3), 16 + i)

            def from_x(i):
                zz = zat(AG_ORDER[i])
                got(buf.at[xat(3), zz, 0], r_sem.at[8 + i])
                if AG_ORDER[i] % 2 == 0:
                    send(xat(3), zz, xd(1), 24 + i)
                got(buf.at[xat(1), zz, 0], r_sem.at[16 + i])
                if AG_ORDER[i] % 2 == 1:
                    send(xat(1), zz, xd(3), 24 + i)

            def to_sibling(i):
                zz = zat(AG_ORDER[i])
                got(buf.at[xat(2), zz, 0], r_sem.at[24 + i])
                bundle = buf.at[:, zz, 0]
                one = rcopy(bundle, bundle, s_sem.at[len(out)], r_sem.at[32 + i], sibling)
                one.start()
                out.append(one)

            send(x, z, zd(1), AG_ORDER.index(-1))
            send(x, z, zd(-1), AG_ORDER.index(1))
            to_x(0)
            for i in range(1, 8):
                s = AG_ORDER[i]
                got(buf.at[x, zat(s), 0], r_sem.at[i])
                if s < 0:
                    send(x, zat(s), zd(1), AG_ORDER.index(s - 1 if s > -3 else 4))
                elif s < 3:
                    send(x, zat(s), zd(-1), AG_ORDER.index(s + 1))
                to_x(i)
                from_x(i - 1)
                if i > 1:
                    to_sibling(i - 2)
            from_x(7)
            to_sibling(6)
            to_sibling(7)
            for i in range(8):
                got(buf.at[:, zat(AG_ORDER[i]), 1], r_sem.at[32 + i])
            for one in out:
                one.wait_send()

        @pl.when(core == 1)
        def _():
            out = []

            def send(ref, device, r):
                one = rcopy(ref, ref, s_sem.at[len(out)], r_sem.at[r], device)
                one.start()
                out.append(one)

            for d in (1, 2, 3):
                send(buf.at[x, z, 1], xd(d), d)
            for d in (1, 2, 3):
                got(buf.at[xat(4 - d), z, 1], r_sem.at[d])
            send(buf.at[:, z, 1], zd(1), 8 + 1)
            send(buf.at[:, z, 1], zd(-1), 16 + 1)
            send(buf.at[:, z, 1], sibling, 32)
            for k in (1, 2, 3, 4):
                for sign in (-1, 1):
                    zz = zat(sign * k)
                    base = 8 if sign == -1 else 16
                    half = buf.at[0:2, zz, 1] if sign == -1 else buf.at[2:4, zz, 1]
                    bundle = buf.at[:, zz, 1]
                    got(bundle if k < 4 else half, r_sem.at[base + k])
                    if k < 4:
                        send(bundle if k < 3 else half, zd(-sign), base + k + 1)
                        send(bundle, sibling, 32 + AG_ORDER.index(sign * k))
            send(buf.at[:, zat(4), 1], sibling, 32 + 7)
            for i in range(8):
                got(buf.at[:, zat(AG_ORDER[i]), 0], r_sem.at[32 + i])
            for one in out:
                one.wait_send()

    gather(acts, ag1_s, ag1_r)
    for copy in w_copies:
        copy.wait()

    bias = jnp.where(xhi == 0, eb[:, :FH], eb[:, FH:])
    for s in range(2):
        for half in range(2):
            rows = slice(384 * half, 384 * half + 384)
            zs = slice(4 * half, 4 * half + 4)
            value = jnp.dot(acts[2 * s, zs].reshape(384, COLS), ew[s, :COLS], preferred_element_type=F32)
            value = value + jnp.dot(acts[2 * s + 1, zs].reshape(384, COLS), ew[s, COLS:], preferred_element_type=F32)
            active = jnp.maximum(value + bias[s:s + 1], 0.0)
            gate[s, rows] = active
            code = (0.5 * active * active).astype(BF16)
            coded[s, rows] = code
            coded_t[s, :, rows] = code.T

    for t in range(2):
        for h in range(2):
            cols = slice(COLS * h, COLS * h + COLS)
            for quarter in range(4):
                rows = slice(192 * quarter, 192 * quarter + 192)
                total = jnp.dot(coded[0, rows], dw[PAIR[0, t], :, cols], preferred_element_type=F32)
                if t == 1:
                    total = total + jnp.dot(coded[1, rows], dw[PAIR[1, 1], :, cols], preferred_element_type=F32)
                part[2 * t + h, 2 * quarter:2 * quarter + 2] = total.astype(BF16).reshape(2, 2, ROWS, COLS)

    sib_sends = []
    for i, s in enumerate(RS_ORDER):
        one = rcopy(part.at[:, zat(s), 1 - core], sib.at[:, zat(s)], rs_s.at[40 + i], rs_r.at[40 + i], sibling)
        one.start()
        sib_sends.append(one)

    def add(dst, terms):
        def some(r, carry):
            sl = pl.ds(pl.multiple_of(r * 16, 16), 16)
            total = terms[0][sl, :].astype(F32)
            for term in terms[1:]:
                total = total + term[sl, :].astype(F32)
            dst[sl, :] = total.astype(dst.dtype)
            return carry

        lax.fori_loop(0, ROWS // 16, some, 0)

    def finish(terms):
        def some(r, carry):
            sl = pl.ds(pl.multiple_of(r * 16, 16), 16)
            total = terms[0][sl, :].astype(F32)
            for term in terms[1:]:
                total = total + term[sl, :].astype(F32)
            errs[x, z, core, sl, :] = (total - tgt[sl, :]).astype(BF16)
            return carry

        lax.fori_loop(0, ROWS // 16, some, 0)

    @pl.when(core == 0)
    def _():
        out = []

        def send(src, r, device):
            one = rcopy(src, recv.at[r], rs_s.at[len(out)], rs_r.at[r], device)
            one.start()
            out.append(one)

        for i, s in enumerate(RS_ORDER):
            zz = zat(s)
            got(sib.at[:, zz], rs_r.at[40 + i])
            unit = part.at[xat(2), zz, 0]
            add(unit, [unit, sib.at[xat(2), zz]])
            send(unit, i, xd(1) if s % 2 == 0 else xd(3))
        for i, s in enumerate(RS_ORDER):
            zz = zat(s)
            got(recv.at[i], rs_r.at[i])
            for d, base, parity in ((1, 8, 0), (3, 16, 1)):
                unit = part.at[xat(d), zz, 0]
                terms = [unit, sib.at[xat(d), zz]]
                if s % 2 == parity:
                    terms.append(recv.at[i])
                add(unit, terms)
                send(unit, base + i, xd(d))
        for i, s in enumerate(RS_ORDER):
            zz = zat(s)
            unit = part.at[x, zz, 0]
            terms = [unit, sib.at[x, zz]]
            got(recv.at[8 + i], rs_r.at[8 + i])
            got(recv.at[16 + i], rs_r.at[16 + i])
            terms += [recv.at[8 + i], recv.at[16 + i]]
            if 0 <= s < 4:
                got(recv.at[24 + (3 - s)], rs_r.at[24 + (3 - s)])
                terms.append(recv.at[24 + (3 - s)])
            if -3 < s <= 0:
                got(recv.at[28 + (2 + s)], rs_r.at[28 + (2 + s)])
                terms.append(recv.at[28 + (2 + s)])
            if s == 0:
                finish(terms)
            else:
                add(unit, terms)
                if s > 0:
                    send(unit, 24 + (4 - s), zd(1))
                else:
                    send(unit, 28 + (3 + s), zd(-1))
        for one in out:
            one.wait_send()

    @pl.when(core == 1)
    def _():
        out = []
        for i, s in enumerate(RS_ORDER):
            zz = zat(s)
            k = abs(s)
            got(sib.at[:, zz], rs_r.at[40 + i])
            up = down = 0
            if 0 <= s < 4:
                up = k + 1
                count = 2 if up == 4 else 4
                got(recv.at[4 * k:4 * k + count], rs_r.at[up])
            if -4 < s <= 0:
                down = k + 1
                count = 2 if down == 4 else 4
                got(recv.at[16 + 4 * k:16 + 4 * k + count], rs_r.at[8 + down])
            for xx in range(4):
                unit = part.at[xx, zz, 1]
                terms = [unit, sib.at[xx, zz]]
                if up and (up < 4 or xx < 2):
                    terms.append(recv.at[4 * k + xx])
                if down and (down < 4 or xx >= 2):
                    terms.append(recv.at[16 + 4 * k + (xx - 2 if down == 4 else xx)])
                add(unit, terms)
            hops = []
            if s == 4:
                hops = [(part.at[0:2, zz, 1], recv.at[12:14], 4, zd(1)), (part.at[2:4, zz, 1], recv.at[28:30], 12, zd(-1))]
            elif s > 0:
                hops = [(part.at[:, zz, 1], recv.at[4 * (k - 1):4 * k], k, zd(1))]
            elif s < 0:
                hops = [(part.at[:, zz, 1], recv.at[16 + 4 * (k - 1):16 + 4 * k], 8 + k, zd(-1))]
            for src, dst, r, device in hops:
                one = rcopy(src, dst, rs_s.at[len(out)], rs_r.at[r], device)
                one.start()
                out.append(one)
        for d in (1, 2, 3):
            one = rcopy(part.at[xat(d), z, 1], recv.at[32 + d], rs_s.at[len(out)], rs_r.at[16 + d], xd(d))
            one.start()
            out.append(one)
        for d in (1, 2, 3):
            got(recv.at[32 + d], rs_r.at[16 + d])
        finish([part.at[x, z, 1], recv.at[33], recv.at[34], recv.at[35]])
        for one in out:
            one.wait_send()

    for one in sib_sends:
        one.wait_send()

    gather(errs, ag2_s, ag2_r)

    y_sends = []

    def start(src, dst, n, d):
        one = rcopy(src, dst, y_s.at[n], y_r.at[n], yd(d))
        one.start()
        y_sends.append(one)

    def first(n, block, one):
        start(block.at[(y + 2) % YN, 0], one.at[0], 4 * n, 1)
        start(block.at[(y + 2) % YN, 1], one.at[1], 4 * n + 1, 3)

    def accumulate(dst, terms, rows):
        def some(r, carry):
            sl = pl.ds(pl.multiple_of(r * 32, 32), 32)
            total = terms[0][sl, :].astype(F32)
            for term in terms[1:]:
                total = total + term[sl, :].astype(F32)
            dst[sl, :] = total.astype(BF16)
            return carry

        lax.fori_loop(0, rows // 32, some, 0)

    def second(n, block, one, two, rows):
        for j, d in ((0, 1), (1, 3)):
            got(one.at[j], y_r.at[4 * n + j])
            mine = block.at[(y + d) % YN, j]
            accumulate(mine, [mine, one.at[j]], rows)
            start(block.at[(y + d) % YN], two.at[j], 4 * n + 2 + j, d)

    def last(n, block, two):
        for j in range(2):
            got(two.at[j], y_r.at[4 * n + 2 + j])

    def dec_grad(s, t):
        p = PAIR[s, t]
        for h in range(2):
            value = jnp.dot(coded_t[s], errs[2 * t + h].reshape(768, COLS), preferred_element_type=F32) * scale
            gdec[p, :, :, :, COLS * h:COLS * h + COLS] = value.astype(BF16).reshape(YN, 2, 32, COLS)
        first(p, gdec.at[p], rone_d.at[p])

    def dcoded(s):
        total_bias = jnp.zeros((1, FH), F32)
        for half in range(2):
            rows = slice(384 * half, 384 * half + 384)
            zs = slice(4 * half, 4 * half + 4)
            value = None
            for t in range(s, 2):
                for h in range(2):
                    term = lax.dot_general(errs[2 * t + h, zs].reshape(384, COLS), dw[PAIR[s, t], :, COLS * h:COLS * h + COLS],
                                           (((1,), (1,)), ((), ())), preferred_element_type=F32)
                    value = term if value is None else value + term
            grad = (value * gate[s, rows]).astype(BF16)
            dpre[s, rows] = grad
            total_bias = total_bias + jnp.sum(grad.astype(F32), axis=0, keepdims=True)
        bsum[s:s + 1, :] = total_bias * scale

    def enc_grad(s):
        for h in range(2):
            value = lax.dot_general(acts[2 * s + h].reshape(768, COLS), dpre[s], (((0,), (0,)), ((), ())), preferred_element_type=F32) * scale
            genc[s, :, h] = value.astype(BF16).reshape(YN, 288, FH)
        first(3 + s, genc.at[s], rone_e.at[s])

    dec_grad(0, 0)
    dcoded(1)
    enc_grad(1)
    dcoded(0)
    enc_grad(0)
    bsum[2:8, :] = jnp.zeros((6, FH), F32)
    b_sends = []
    for d in (1, 2, 3):
        one = rcopy(bsum, bland.at[d], b_s.at[d], b_r.at[d], yd(d))
        one.start()
        b_sends.append(one)
    second(0, gdec.at[0], rone_d.at[0], rtwo_d.at[0], 32)
    dec_grad(0, 1)
    second(4, genc.at[1], rone_e.at[1], rtwo_e.at[1], 288)
    dec_grad(1, 1)
    second(3, genc.at[0], rone_e.at[0], rtwo_e.at[0], 288)
    second(1, gdec.at[1], rone_d.at[1], rtwo_d.at[1], 32)
    second(2, gdec.at[2], rone_d.at[2], rtwo_d.at[2], 32)

    def dec_out(p):
        last(p, gdec.at[p], rtwo_d.at[p])
        for j in range(2):
            accumulate(gd_out.at[p, 32 * j:32 * j + 32], [gdec.at[p, y, j], rtwo_d.at[p, 0, j], rtwo_d.at[p, 1, j]], 32)

    def enc_out(s):
        last(3 + s, genc.at[s], rtwo_e.at[s])
        for j in range(2):
            mine = genc.at[s, y, j]
            accumulate(mine, [mine, rtwo_e.at[s, 0, j], rtwo_e.at[s, 1, j]], 288)
        one = rcopy(genc.at[s, y, 1 - xhi], swap.at[s], sw_s.at[s], sw_r.at[s], xd(2))
        one.start()
        return one

    dec_out(0)
    swaps = [enc_out(1), enc_out(0)]
    dec_out(1)
    dec_out(2)
    for d in (1, 2, 3):
        got(bland.at[d], b_r.at[d])
    gb_out[...] = bsum[...] + bland[1] + bland[2] + bland[3]
    for s in (1, 0):
        got(swap.at[s], sw_r.at[s])

        @pl.when(xhi == 0)
        def _():
            ge_out[s, :, :FH] = genc[s, y, 0]
            ge_out[s, :, FH:] = swap[s]

        @pl.when(xhi == 1)
        def _():
            ge_out[s, :, :FH] = swap[s]
            ge_out[s, :, FH:] = genc[s, y, 1]

    for one in sends + y_sends + b_sends + swaps:
        one.wait_send()


def shards(acts_in, targets, enc_weight, enc_bias, dec_weight):
    both = jnp.stack([acts_in, targets])
    both = both.reshape(2, TD, 4, COLS).transpose(0, 2, 1, 3)
    both = jnp.pad(both, ((0, 0), (0, 0), (0, 16 - TD), (0, 0)))
    dma = pltpu.SemaphoreType.DMA
    unit = (ROWS, COLS)
    vmem = pl.BlockSpec(memory_space=pltpu.VMEM)
    hbm = pl.BlockSpec(memory_space=pl.ANY)
    ge, gb, gd = pl.pallas_call(
        kernel,
        out_shape=(
            jax.ShapeDtypeStruct((2, 288, 512), BF16),
            jax.ShapeDtypeStruct((8, FH), F32),
            jax.ShapeDtypeStruct((3, 64, 2304), BF16),
        ),
        in_specs=[vmem, vmem, hbm, hbm],
        out_specs=(vmem, vmem, vmem),
        scratch_shapes=[
            pltpu.VMEM((2, XN, 16, COLS), BF16),
            pltpu.VMEM((XN, ZN, 2) + unit, BF16),
            pltpu.VMEM(unit, F32),
            pltpu.VMEM((XN, ZN, 2) + unit, BF16),
            pltpu.VMEM((2, 2304, FH), BF16),
            pltpu.VMEM((3, FH, 2304), BF16),
            pltpu.VMEM((2, 768, FH), F32),
            pltpu.VMEM((2, 768, FH), BF16),
            pltpu.VMEM((2, FH, 768), BF16),
            pltpu.VMEM((2, 768, FH), BF16),
            pltpu.VMEM((XN, ZN, 2) + unit, BF16),
            pltpu.VMEM((XN, ZN) + unit, BF16),
            pltpu.VMEM((36,) + unit, BF16),
            pltpu.VMEM((3, YN, 2, 32, 2304), BF16),
            pltpu.VMEM((2, YN, 2, 288, FH), BF16),
            pltpu.VMEM((3, 2, 32, 2304), BF16),
            pltpu.VMEM((2, 2, 288, FH), BF16),
            pltpu.VMEM((3, 2, 2, 32, 2304), BF16),
            pltpu.VMEM((2, 2, 2, 288, FH), BF16),
            pltpu.VMEM((2, 288, FH), BF16),
            pltpu.VMEM((8, FH), F32),
            pltpu.VMEM((4, 8, FH), F32),
            dma((2,)), dma((4,)), dma((4,)),
            dma((40,)), dma((40,)), dma((48,)), dma((48,)), dma((40,)), dma((40,)),
            dma((20,)), dma((20,)), dma((4,)), dma((4,)), dma((2,)), dma((2,)),
        ],
        compiler_params=pltpu.CompilerParams(collective_id=0, has_side_effects=True, vmem_limit_bytes=67_000_000),
    )(both, enc_bias, enc_weight, dec_weight)
    y = lax.axis_index("tok") % YN
    gb = lax.dynamic_slice(gb, (0, y * 64), (2, 64))
    return ge, gb, gd


def solution(mesh):
    return jax.shard_map(
        shards,
        mesh=mesh,
        in_specs=(
            P(("tok", "feat"), None, None),
            P(("tok", "feat"), None, None),
            P(None, None, "feat"),
            P(None, "feat"),
            P(None, "feat", None),
        ),
        out_specs=(
            P(None, "tok", "feat"),
            P(None, ("feat", "tok")),
            P(None, ("feat", "tok"), None),
        ),
        check_vma=False,
    )
```

```python
import math

import jax
import jax.numpy as jnp
from jax import lax
from jax.experimental import pallas as pl
from jax.experimental.pallas import tpu as pltpu
from jax.sharding import PartitionSpec as P

MESH = pl.DeviceIdType.MESH
F32 = jnp.float32
BF16 = jnp.bfloat16
XN, ZN, YN = 4, 8, 4
TD = 12
ROWS = XN * TD
COLS = 1152
MAIN, REST = 512, 128
BASE = (0, MAIN + REST)
FH = 256
AG_ORDER = (0, -1, 1, -2, 2, -3, 3, 4)
RS_ORDER = (4, 3, -3, 2, -2, 1, -1, 0)
AG_INDEX = {s: i for i, s in enumerate(AG_ORDER)}
LATE = 3
PAIR = {(0, 0): 0, (0, 1): 1, (1, 1): 2}


def kernel(inp, eb, ew_hbm, dw_hbm, ge_out, gb_out, gd_out,
           land, acts, tgt, errs, ew, dw, gate, coded, coded_t, dpre, part, sib, recv,
           gdec, genc, rone_d, rone_e, rtwo_d, rtwo_e, swap, bsum, bland,
           wsem, a2a_s, a2a_r, ring_s, ring_r, y_s, y_r, b_s, b_r, sw_s, sw_r):
    fi = lax.axis_index("feat")
    ti = lax.axis_index("tok")
    core = fi % 2
    z = (fi // 2) % ZN
    xlo = fi // (2 * ZN)
    y = ti % YN
    xhi = ti // YN
    x = 2 * xhi + xlo
    scale = 1.0 / math.sqrt(3072.0)

    def dev(xx, zz, yy, cc):
        return ((xx % 2) * (2 * ZN) + zz * 2 + cc, (xx // 2) * YN + yy)

    def xd(d):
        return dev((x + d) % XN, z, y, core)

    def zd(d):
        return dev(x, (z + d + ZN) % ZN, y, core)

    def yd(d):
        return dev(x, z, (y + d) % YN, core)

    def zat(s):
        return (z + s + ZN) % ZN

    def xat(d):
        return (x + d) % XN

    sibling = dev(x, z, y, 1 - core)

    def rcopy(src, dst, ssem, rsem, device):
        return pltpu.make_async_remote_copy(src_ref=src, dst_ref=dst, send_sem=ssem, recv_sem=rsem, device_id=device, device_id_type=MESH)

    def got(dst, rsem):
        rcopy(dst, dst, rsem, rsem, sibling).wait_recv()

    bsum[...] = jnp.zeros_like(bsum)
    fo = pl.multiple_of(xhi * FH, FH)
    w_copies = [pltpu.make_async_copy(ew_hbm.at[:, :, pl.ds(fo, FH)], ew, wsem.at[0]),
                pltpu.make_async_copy(dw_hbm.at[:, pl.ds(fo, FH), :], dw, wsem.at[1])]
    for copy in w_copies:
        copy.start()

    barrier = pltpu.get_barrier_semaphore()
    partners = [sibling] + [xd(d) for d in (1, 2, 3)] + [zd(1), zd(-1)] + [yd(d) for d in (1, 2, 3)]
    for partner in partners:
        pl.semaphore_signal(barrier, inc=1, device_id=partner, device_id_type=MESH)
    pl.semaphore_wait(barrier, len(partners))

    sends = []
    for d in (1, 2, 3):
        send = rcopy(inp.at[:, xat(d)], land.at[:, d], a2a_s.at[d], a2a_r.at[d], xd(d))
        send.start()
        sends.append(send)
    land[:, 0] = inp[:, x]
    row = lax.broadcasted_iota(jnp.int32, (ROWS, XN * 16), 0)
    col = lax.broadcasted_iota(jnp.int32, (ROWS, XN * 16), 1)
    source = (x + XN - col // 16) % XN
    place = jnp.where((row == TD * source + col % 16) & (col % 16 < TD), 1.0, 0.0).astype(BF16)
    for d in (1, 2, 3):
        got(land.at[:, d], a2a_r.at[d])
    acts[x, z, core] = jnp.dot(place, land[0].reshape(XN * 16, COLS), preferred_element_type=F32).astype(BF16)
    tgt[...] = jnp.dot(place, land[1].reshape(XN * 16, COLS), preferred_element_type=F32)

    done = []

    def each(zero, one):
        pl.when(core == 0)(zero)
        pl.when(core == 1)(one)

    sent = ([], [])

    def gather(buf, lo, hi, stage):
        ss, rr = ring_s.at[stage], ring_r.at[stage]
        count = [0, 0]

        def send(c, ref, like, r, device):
            rcopy(ref, ref, ss.at[count[c]], rr.at[r], device).start()
            sent[c].append((like, ring_s, (stage, count[c])))
            count[c] += 1

        def like_unit():
            return buf.at[0, 0, 0, :, lo:hi]

        def like_bundle():
            return buf.at[:, 0, 0, :, lo:hi]


        def unit(c, xx, s):
            return buf.at[xx, zat(s), c, :, lo:hi]

        def bundle(c, s):
            return buf.at[:, zat(s), c, :, lo:hi]

        def to_x(i):
            s = AG_ORDER[i]
            send(0, unit(0, x, s), like_unit, 8 + i, xd(1))
            send(0, unit(0, x, s), like_unit, 16 + i, xd(3))

        def from_x(i):
            s = AG_ORDER[i]
            got(unit(0, xat(3), s), rr.at[8 + i])
            if s % 2 == 0:
                send(0, unit(0, xat(3), s), like_unit, 24 + i, xd(1))
            got(unit(0, xat(1), s), rr.at[16 + i])
            if s % 2 == 1:
                send(0, unit(0, xat(1), s), like_unit, 24 + i, xd(3))

        def to_sibling(i):
            s = AG_ORDER[i]
            got(unit(0, xat(2), s), rr.at[24 + i])
            send(0, bundle(0, s), like_bundle, 36 + i, sibling)

        def zero(j):
            if j == 0:
                send(0, unit(0, x, 0), like_unit, AG_INDEX[-1], zd(1))
                send(0, unit(0, x, 0), like_unit, AG_INDEX[1], zd(-1))
                to_x(0)
            elif j < 8:
                s = AG_ORDER[j]
                got(unit(0, x, s), rr.at[j])
                if s < 0:
                    send(0, unit(0, x, s), like_unit, AG_INDEX[s - 1] if s > -3 else 7, zd(1))
                elif s < 3:
                    send(0, unit(0, x, s), like_unit, AG_INDEX[s + 1], zd(-1))
                to_x(j)
            if LATE <= j < LATE + 8:
                from_x(j - LATE)
            if 2 * LATE <= j < 2 * LATE + 8:
                to_sibling(j - 2 * LATE)

        def one(j):
            if j == 0:
                for d in (1, 2, 3):
                    send(1, unit(1, x, 0), like_unit, d, xd(d))
            elif j == 1:
                for d in (0, 1, 3, 2):
                    if d:
                        got(unit(1, xat(4 - d), 0), rr.at[d])
                    send(1, unit(1, xat(4 - d), 0), like_unit, 4 + d, zd(1))
                    send(1, unit(1, xat(4 - d), 0), like_unit, 20 + d, zd(-1))
                send(1, bundle(1, 0), like_bundle, 36, sibling)
            elif 2 <= j < 6:
                k = j - 1
                for d in (0, 1, 3, 2):
                    for sign, base in ((-1, 4), (1, 20)):
                        if k == 4 and (d < 2) != (sign < 0):
                            continue
                        part_ = unit(1, xat(4 - d), sign * k)
                        got(part_, rr.at[base + 4 * (k - 1) + d])
                        if k < 3 or (k == 3 and (d < 2) == (sign < 0)):
                            send(1, part_, like_unit, base + 4 * k + d, zd(-sign))
                send(1, bundle(1, -k), like_bundle, 36 + AG_INDEX.get(-k, 7), sibling)
                if k < 4:
                    send(1, bundle(1, k), like_bundle, 36 + AG_INDEX[k], sibling)

        for j in range(8 + 2 * LATE):
            each(lambda: zero(j), lambda: one(j))
            yield
        for i in range(8):
            got(buf.at[:, zat(AG_ORDER[i]), 1 - core, :, lo:hi], rr.at[36 + i])
        yield

    def halves(lo, hi, stage, group):
        ss, rr = ring_s.at[stage], ring_r.at[stage]
        for i in group:
            zz = zat(RS_ORDER[i])
            one = rcopy(part.at[:, zz, 1 - core, :, lo:hi], sib.at[:, zz, :, lo:hi], ss.at[44 + i], rr.at[36 + i], sibling)
            one.start()
            done.append(one)

    def total_of(terms):
        total = terms[0][...].astype(F32)
        for term in terms[1:]:
            total = total + term[...].astype(F32)
        return total

    def scatter(lo, hi, stage):
        ss, rr = ring_s.at[stage], ring_r.at[stage]
        count = [0, 0]

        def slot(r):
            return recv.at[r, :, lo:hi]

        def send(c, src, r, device):
            rcopy(src, slot(r), ss.at[count[c]], rr.at[r], device).start()
            sent[c].append((lambda: slot(0), ring_s, (stage, count[c])))
            count[c] += 1

        def mine(c, xx, s):
            return part.at[xx, zat(s), c, :, lo:hi]

        def theirs(xx, s):
            return sib.at[xx, zat(s), :, lo:hi]

        def add(dst, terms):
            dst[...] = total_of(terms).astype(BF16)

        def finish(c, terms):
            errs[x, z, c, :, lo:hi] = (total_of(terms) - tgt[:, lo:hi]).astype(BF16)

        def across(i):
            s = RS_ORDER[i]
            got(sib.at[:, zat(s), :, lo:hi], rr.at[36 + i])
            add(mine(0, xat(2), s), [mine(0, xat(2), s), theirs(xat(2), s)])
            send(0, mine(0, xat(2), s), i, xd(1) if s % 2 == 0 else xd(3))

        def beside(i):
            s = RS_ORDER[i]
            got(slot(i), rr.at[i])
            for d, base, parity in ((1, 8, 0), (3, 16, 1)):
                terms = [mine(0, xat(d), s), theirs(xat(d), s)]
                if s % 2 == parity:
                    terms.append(slot(i))
                add(mine(0, xat(d), s), terms)
                send(0, mine(0, xat(d), s), base + i, xd(d))

        def along(i):
            s = RS_ORDER[i]
            k = abs(s)
            got(slot(8 + i), rr.at[8 + i])
            got(slot(16 + i), rr.at[16 + i])
            terms = [mine(0, x, s), theirs(x, s), slot(8 + i), slot(16 + i)]
            if 0 <= s < 4:
                got(slot(24 + 3 - k), rr.at[24 + 3 - k])
                terms.append(slot(24 + 3 - k))
            if -3 < s <= 0:
                got(slot(28 + 3 - k), rr.at[28 + 3 - k])
                terms.append(slot(28 + 3 - k))
            if s == 0:
                finish(0, terms)
                return
            add(mine(0, x, s), terms)
            if s > 0:
                send(0, mine(0, x, s), 24 + 4 - k, zd(1))
            else:
                send(0, mine(0, x, s), 28 + 4 - k, zd(-1))

        def zero(j):
            if j < 8:
                across(j)
            if LATE <= j < LATE + 8:
                beside(j - LATE)
            if 2 * LATE <= j < 2 * LATE + 8:
                along(j - 2 * LATE)

        def one(j):
            if j < 8:
                s = RS_ORDER[j]
                k = abs(s)
                got(sib.at[:, zat(s), :, lo:hi], rr.at[36 + j])
                for d in (2, 1, 3, 0):
                    xx = xat(d)
                    terms = [mine(1, xx, s), theirs(xx, s)]
                    for here, base in ((0 <= s < 4 and (k < 3 or d < 2), 0), (-4 < s <= 0 and (k < 3 or d >= 2), 16)):
                        if here:
                            got(slot(base + 4 * k + d), rr.at[base + 4 * k + d])
                            terms.append(slot(base + 4 * k + d))
                    add(mine(1, xx, s), terms)
                    if s == 4:
                        send(1, mine(1, xx, s), (0 if d < 2 else 16) + 12 + d, zd(1) if d < 2 else zd(-1))
                    elif s > 0:
                        send(1, mine(1, xx, s), 4 * (k - 1) + d, zd(1))
                    elif s < 0:
                        send(1, mine(1, xx, s), 16 + 4 * (k - 1) + d, zd(-1))
                    elif d:
                        send(1, mine(1, xx, s), 32 + d, xd(d))
            elif j == 7 + 2 * LATE:
                terms = [mine(1, x, 0)]
                for d in (1, 2, 3):
                    got(slot(32 + d), rr.at[32 + d])
                    terms.append(slot(32 + d))
                finish(1, terms)

        for j in range(8 + 2 * LATE):
            each(lambda: zero(j), lambda: one(j))
            yield

    def pieces(buf, layer, zs):
        lo = BASE[layer]
        rows = 768 if zs == slice(0, 8) else 384
        for xx in range(4):
            yield buf[xx, zs, :, :, lo:lo + MAIN].reshape(rows, MAIN), MAIN * xx
        rest = [buf[2 * layer + j, zs, :, :, MAIN:MAIN + REST].reshape(rows, REST) for j in range(2)]
        yield jnp.concatenate(rest, axis=1), 4 * MAIN

    bias = jnp.where(xhi == 0, eb[:, :FH], eb[:, FH:])

    def encode(s, half):
        rows = slice(384 * half, 384 * half + 384)
        zs = slice(4 * half, 4 * half + 4)
        value = bias[s:s + 1]
        for cols, first in pieces(acts, s, zs):
            value = value + jnp.dot(cols, ew[s, first:first + cols.shape[1]], preferred_element_type=F32)
        active = jnp.maximum(value, 0.0)
        gate[s, rows] = active
        code = (0.5 * active * active).astype(BF16)
        coded[s, zs] = code.reshape(4, 96, FH)
        coded_t[s, :, rows] = code.T

    def decode(t, xx, group):
        width = MAIN if xx < 4 else 2 * REST
        total = None
        for s in range(t + 1):
            codes = jnp.concatenate([coded[s, zat(RS_ORDER[i])] for i in group], axis=0)
            term = jnp.dot(codes, dw[PAIR[s, t], :, MAIN * xx:MAIN * xx + width], preferred_element_type=F32)
            total = term if total is None else total + term
        total = total.astype(BF16)
        for n, i in enumerate(group):
            rows = total[96 * n:96 * n + 96]
            zz = zat(RS_ORDER[i])
            if xx < 4:
                part[xx, zz, :, :, BASE[t]:BASE[t] + MAIN] = rows.reshape(2, ROWS, MAIN)
            else:
                for j in range(2):
                    part[2 * t + j, zz, :, :, MAIN:MAIN + REST] = rows[:, REST * j:REST * j + REST].reshape(2, ROWS, REST)

    def start(src, dst, n, d):
        one = rcopy(src, dst, y_s.at[n], y_r.at[n], yd(d))
        one.start()
        done.append(one)

    def first(n, block, one):
        start(block.at[(y + 2) % YN, 0], one.at[0], 4 * n, 1)
        start(block.at[(y + 2) % YN, 1], one.at[1], 4 * n + 1, 3)

    def accumulate(dst, terms, rows):
        def some(r, carry):
            sl = pl.ds(pl.multiple_of(r * 32, 32), 32)
            total = terms[0][sl, :].astype(F32)
            for term in terms[1:]:
                total = total + term[sl, :].astype(F32)
            dst[sl, :] = total.astype(BF16)
            return carry

        lax.fori_loop(0, rows // 32, some, 0)

    def second(n, block, one, two, rows):
        for j, d in ((0, 1), (1, 3)):
            got(one.at[j], y_r.at[4 * n + j])
            mine = block.at[(y + d) % YN, j]
            accumulate(mine, [mine, one.at[j]], rows)
            start(block.at[(y + d) % YN], two.at[j], 4 * n + 2 + j, d)

    def last(n, two):
        for j in range(2):
            got(two.at[j], y_r.at[4 * n + 2 + j])

    whole = slice(0, 8)

    def dec_grad(s, t):
        p = PAIR[s, t]
        for cols, at in pieces(errs, t, whole):
            width = cols.shape[1]
            value = jnp.dot(coded_t[s], cols, preferred_element_type=F32) * scale
            gdec[p, :, :, :, at:at + width] = value.astype(BF16).reshape(YN, 2, 32, width)
        first(p, gdec.at[p], rone_d.at[p])

    def dcoded(s):
        total_bias = jnp.zeros((1, FH), F32)
        for half in range(2):
            rows = slice(384 * half, 384 * half + 384)
            value = None
            for t in range(s, 2):
                for cols, at in pieces(errs, t, slice(4 * half, 4 * half + 4)):
                    term = lax.dot_general(cols, dw[PAIR[s, t], :, at:at + cols.shape[1]],
                                           (((1,), (1,)), ((), ())), preferred_element_type=F32)
                    value = term if value is None else value + term
            grad = (value * gate[s, rows]).astype(BF16)
            dpre[s, rows] = grad
            total_bias = total_bias + jnp.sum(grad.astype(F32), axis=0, keepdims=True)
        bsum[s:s + 1, :] = total_bias * scale

    def enc_grad(s):
        for cols, at in pieces(acts, s, whole):
            value = lax.dot_general(cols, dpre[s], (((0,), (0,)), ((), ())), preferred_element_type=F32) * scale
            value = value.astype(BF16)
            row, end = at, at + cols.shape[1]
            while row < end:
                stop = min(end, (row // 288 + 1) * 288)
                owner, place_ = row // 288, row % 288
                genc[s, owner % YN, owner // YN, place_:place_ + stop - row] = value[row - at:stop - at]
                row = stop
        first(3 + s, genc.at[s], rone_e.at[s])

    def dec_second(p):
        second(p, gdec.at[p], rone_d.at[p], rtwo_d.at[p], 32)

    def enc_second(s):
        second(3 + s, genc.at[s], rone_e.at[s], rtwo_e.at[s], 288)

    def dec_out(p):
        last(p, rtwo_d.at[p])
        for j in range(2):
            accumulate(gd_out.at[p, 32 * j:32 * j + 32], [gdec.at[p, y, j], rtwo_d.at[p, 0, j], rtwo_d.at[p, 1, j]], 32)

    def enc_out(s):
        last(3 + s, rtwo_e.at[s])
        for j in range(2):
            mine = genc.at[s, y, j]
            accumulate(mine, [mine, rtwo_e.at[s, 0, j], rtwo_e.at[s, 1, j]], 288)
        one = rcopy(genc.at[s, y, 1 - xhi], swap.at[s], sw_s.at[s], sw_r.at[s], xd(2))
        one.start()
        done.append(one)

    def turn(*steps):
        more = [next(one, "end") is None for one in steps]
        return more[0]

    inputs = gather(acts, 0, COLS, 0)
    while turn(inputs):
        pass
    for copy in w_copies:
        copy.wait()
    for s in range(2):
        for half in range(2):
            encode(s, half)
    one, zero = (MAIN, COLS), (0, MAIN)
    for group in (range(4), range(4, 8)):
        for xx in range(5):
            decode(1, xx, group)
        decode(0, 4, group)
        halves(*one, 1, group)
    for group in (range(4), range(4, 8)):
        for xx in range(4):
            decode(0, xx, group)
        halves(*zero, 2, group)
    early = scatter(*one, 1)
    while turn(early):
        pass
    early, late = gather(errs, *one, 3), scatter(*zero, 2)
    while turn(early, late):
        pass
    while turn(late):
        pass
    later = gather(errs, *zero, 4)
    turn(later)
    dec_grad(0, 1)
    turn(later)
    dec_grad(1, 1)
    turn(later)
    dec_second(1)
    turn(later)
    dec_second(2)
    turn(later)
    dcoded(1)
    turn(later)
    enc_grad(1)
    turn(later)
    turn(later)
    turn(later)
    enc_second(1)
    while turn(later):
        pass
    dcoded(0)
    enc_grad(0)
    dec_grad(0, 0)
    for d in (1, 2, 3):
        one = rcopy(bsum, bland.at[d], b_s.at[d], b_r.at[d], yd(d))
        one.start()
        done.append(one)
    enc_second(0)
    dec_second(0)
    dec_out(1)
    dec_out(2)
    enc_out(1)
    enc_out(0)
    for d in (1, 2, 3):
        got(bland.at[d], b_r.at[d])
    total = bsum[...] + bland[1] + bland[2] + bland[3]
    own = jnp.where(y == 0, total[:, :64], 0.0)
    for n in range(1, YN):
        own = own + jnp.where(y == n, total[:, 64 * n:64 * n + 64], 0.0)
    gb_out[...] = own[:2]
    dec_out(0)
    for s in (1, 0):
        got(swap.at[s], sw_r.at[s])

        @pl.when(xhi == 0)
        def _():
            ge_out[s, :, :FH] = genc[s, y, 0]
            ge_out[s, :, FH:] = swap[s]

        @pl.when(xhi == 1)
        def _():
            ge_out[s, :, :FH] = swap[s]
            ge_out[s, :, FH:] = genc[s, y, 1]

    for one in sends + done:
        one.wait_send()

    def drain(c):
        for like, sems, at in sent[c]:
            rcopy(like(), like(), sems.at[at], sems.at[at], sibling).wait_send()

    each(lambda: drain(0), lambda: drain(1))


def shards(acts_in, targets, enc_weight, enc_bias, dec_weight):
    both = jnp.stack([acts_in, targets])
    main = both[..., :4 * MAIN].reshape(2, TD, 2, 4, MAIN)
    rest = both[..., 4 * MAIN:].reshape(2, TD, 4, REST)
    both = jnp.concatenate([main[:, :, 0], rest, main[:, :, 1]], axis=-1).transpose(0, 2, 1, 3)
    both = jnp.pad(both, ((0, 0), (0, 0), (0, 16 - TD), (0, 0)))
    dma = pltpu.SemaphoreType.DMA
    unit = (ROWS, COLS)
    vmem = pl.BlockSpec(memory_space=pltpu.VMEM)
    hbm = pl.BlockSpec(memory_space=pl.ANY)
    ge, gb, gd = pl.pallas_call(
        kernel,
        out_shape=(
            jax.ShapeDtypeStruct((2, 288, 512), BF16),
            jax.ShapeDtypeStruct((2, 64), F32),
            jax.ShapeDtypeStruct((3, 64, 2304), BF16),
        ),
        in_specs=[vmem, vmem, hbm, hbm],
        out_specs=(vmem, vmem, vmem),
        scratch_shapes=[
            pltpu.VMEM((2, XN, 16, COLS), BF16),
            pltpu.VMEM((XN, ZN, 2) + unit, BF16),
            pltpu.VMEM(unit, F32),
            pltpu.VMEM((XN, ZN, 2) + unit, BF16),
            pltpu.VMEM((2, 2304, FH), BF16),
            pltpu.VMEM((3, FH, 2304), BF16),
            pltpu.VMEM((2, 768, FH), F32),
            pltpu.VMEM((2, ZN, 96, FH), BF16),
            pltpu.VMEM((2, FH, 768), BF16),
            pltpu.VMEM((2, 768, FH), BF16),
            pltpu.VMEM((XN, ZN, 2) + unit, BF16),
            pltpu.VMEM((XN, ZN) + unit, BF16),
            pltpu.VMEM((36,) + unit, BF16),
            pltpu.VMEM((3, YN, 2, 32, 2304), BF16),
            pltpu.VMEM((2, YN, 2, 288, FH), BF16),
            pltpu.VMEM((3, 2, 32, 2304), BF16),
            pltpu.VMEM((2, 2, 288, FH), BF16),
            pltpu.VMEM((3, 2, 2, 32, 2304), BF16),
            pltpu.VMEM((2, 2, 2, 288, FH), BF16),
            pltpu.VMEM((2, 288, FH), BF16),
            pltpu.VMEM((8, FH), F32),
            pltpu.VMEM((4, 8, FH), F32),
            dma((2,)), dma((4,)), dma((4,)),
            dma((5, 52)), dma((5, 44)),
            dma((20,)), dma((20,)), dma((4,)), dma((4,)), dma((2,)), dma((2,)),
        ],
        compiler_params=pltpu.CompilerParams(collective_id=0, has_side_effects=True, vmem_limit_bytes=67_000_000),
    )(both, enc_bias, enc_weight, dec_weight)
    return ge, gb, gd


def solution(mesh):
    return jax.shard_map(
        shards,
        mesh=mesh,
        in_specs=(
            P(("tok", "feat"), None, None),
            P(("tok", "feat"), None, None),
            P(None, None, "feat"),
            P(None, "feat"),
            P(None, "feat", None),
        ),
        out_specs=(
            P(None, "tok", "feat"),
            P(None, ("feat", "tok")),
            P(None, ("feat", "tok"), None),
        ),
        check_vma=False,
    )
```

```python
import math

import jax
import jax.numpy as jnp
from jax import lax
from jax.experimental import pallas as pl
from jax.experimental.pallas import tpu as pltpu
from jax.sharding import PartitionSpec as P

MESH = pl.DeviceIdType.MESH
F32 = jnp.float32
BF16 = jnp.bfloat16
XN, ZN, YN = 4, 8, 4
TD = 12
ROWS = XN * TD
COLS = 1152
MAIN, REST = 512, 128
BASE = (0, MAIN + REST)
FH = 256
AG_ORDER = (0, -1, 1, -2, 2, -3, 3, 4)
RS_ORDER = (4, 3, -3, 2, -2, 1, -1, 0)
AG_INDEX = {s: i for i, s in enumerate(AG_ORDER)}
LATE = 3
PAIR = {(0, 0): 0, (0, 1): 1, (1, 1): 2}


def kernel(inp, eb, ew_hbm, dw_hbm, ge_out, gb_out, gd_out,
           land, acts, tgt, errs, ew, dw, gate, coded, coded_t, dpre, part, sib, recv,
           gdec, genc, rone_d, rone_e, rtwo_d, rtwo_e, swap, bsum, bland,
           wsem, a2a_s, a2a_r, ring_s, ring_r, y_s, y_r, b_s, b_r, sw_s, sw_r):
    fi = lax.axis_index("feat")
    ti = lax.axis_index("tok")
    core = fi % 2
    z = (fi // 2) % ZN
    xlo = fi // (2 * ZN)
    y = ti % YN
    xhi = ti // YN
    x = 2 * xhi + xlo
    scale = 1.0 / math.sqrt(3072.0)

    def dev(xx, zz, yy, cc):
        return ((xx % 2) * (2 * ZN) + zz * 2 + cc, (xx // 2) * YN + yy)

    def xd(d):
        return dev((x + d) % XN, z, y, core)

    def zd(d):
        return dev(x, (z + d + ZN) % ZN, y, core)

    def yd(d):
        return dev(x, z, (y + d) % YN, core)

    def zat(s):
        return (z + s + ZN) % ZN

    def xat(d):
        return (x + d) % XN

    sibling = dev(x, z, y, 1 - core)

    def rcopy(src, dst, ssem, rsem, device):
        return pltpu.make_async_remote_copy(src_ref=src, dst_ref=dst, send_sem=ssem, recv_sem=rsem, device_id=device, device_id_type=MESH)

    def got(dst, rsem):
        rcopy(dst, dst, rsem, rsem, sibling).wait_recv()

    bsum[...] = jnp.zeros_like(bsum)
    fo = pl.multiple_of(xhi * FH, FH)
    w_copies = [pltpu.make_async_copy(ew_hbm.at[:, :, pl.ds(fo, FH)], ew, wsem.at[0]),
                pltpu.make_async_copy(dw_hbm.at[:, pl.ds(fo, FH), :], dw, wsem.at[1])]
    for copy in w_copies:
        copy.start()

    barrier = pltpu.get_barrier_semaphore()
    partners = [sibling] + [xd(d) for d in (1, 2, 3)] + [zd(d) for d in (1, -1, 2, -2)] + [yd(d) for d in (1, 2, 3)]
    for partner in partners:
        pl.semaphore_signal(barrier, inc=1, device_id=partner, device_id_type=MESH)
    pl.semaphore_wait(barrier, len(partners))

    sends = []
    for d in (1, 2, 3):
        send = rcopy(inp.at[:, xat(d)], land.at[:, d], a2a_s.at[d], a2a_r.at[d], xd(d))
        send.start()
        sends.append(send)
    land[:, 0] = inp[:, x]
    row = lax.broadcasted_iota(jnp.int32, (ROWS, XN * 16), 0)
    col = lax.broadcasted_iota(jnp.int32, (ROWS, XN * 16), 1)
    source = (x + XN - col // 16) % XN
    place = jnp.where((row == TD * source + col % 16) & (col % 16 < TD), 1.0, 0.0).astype(BF16)
    for d in (1, 2, 3):
        got(land.at[:, d], a2a_r.at[d])
    acts[x, z, core] = jnp.dot(place, land[0].reshape(XN * 16, COLS), preferred_element_type=F32).astype(BF16)
    tgt[...] = jnp.dot(place, land[1].reshape(XN * 16, COLS), preferred_element_type=F32)

    done = []

    def each(zero, one):
        pl.when(core == 0)(zero)
        pl.when(core == 1)(one)

    sent = ([], [])

    def gather(buf, lo, hi, stage):
        ss, rr = ring_s.at[stage], ring_r.at[stage]
        count = [0, 0]

        def send(c, ref, like, r, device):
            rcopy(ref, ref, ss.at[count[c]], rr.at[r], device).start()
            sent[c].append((like, ring_s, (stage, count[c])))
            count[c] += 1

        def like_unit():
            return buf.at[0, 0, 0, :, lo:hi]

        def like_bundle():
            return buf.at[:, 0, 0, :, lo:hi]


        def unit(c, xx, s):
            return buf.at[xx, zat(s), c, :, lo:hi]

        def bundle(c, s):
            return buf.at[:, zat(s), c, :, lo:hi]

        def to_x(i):
            for d, base in ((2, 24), (1, 8), (3, 16)):
                send(0, unit(0, x, AG_ORDER[i]), like_unit, base + i, xd(d))

        def to_sibling(i):
            s = AG_ORDER[i]
            for d, base in ((3, 8), (1, 16), (2, 24)):
                got(unit(0, xat(d), s), rr.at[base + i])
            send(0, bundle(0, s), like_bundle, 36 + i, sibling)

        onward = {0: ((-1, 1), (1, -1), (-2, 2), (2, -2)), -2: ((-3, 1),), 2: ((3, -1), (4, -2))}

        def zero(j):
            if j < 8:
                s = AG_ORDER[j]
                if j:
                    got(unit(0, x, s), rr.at[j])
                for seen, d in onward.get(s, ()):
                    send(0, unit(0, x, s), like_unit, AG_INDEX[seen], zd(d))
                to_x(j)
            if LATE <= j < LATE + 8:
                to_sibling(j - LATE)

        def one(j):
            if j == 0:
                for d in (1, 2, 3):
                    send(1, unit(1, x, 0), like_unit, d, xd(d))
            elif j == 1:
                for d in (0, 1, 3, 2):
                    if d:
                        got(unit(1, xat(4 - d), 0), rr.at[d])
                    send(1, unit(1, xat(4 - d), 0), like_unit, 4 + d, zd(1))
                    send(1, unit(1, xat(4 - d), 0), like_unit, 20 + d, zd(-1))
                send(1, bundle(1, 0), like_bundle, 36, sibling)
            elif 2 <= j < 6:
                k = j - 1
                for d in (0, 1, 3, 2):
                    for sign, base in ((-1, 4), (1, 20)):
                        if k == 4 and (d < 2) != (sign < 0):
                            continue
                        part_ = unit(1, xat(4 - d), sign * k)
                        got(part_, rr.at[base + 4 * (k - 1) + d])
                        if k < 3 or (k == 3 and (d < 2) == (sign < 0)):
                            send(1, part_, like_unit, base + 4 * k + d, zd(-sign))
                send(1, bundle(1, -k), like_bundle, 36 + AG_INDEX.get(-k, 7), sibling)
                if k < 4:
                    send(1, bundle(1, k), like_bundle, 36 + AG_INDEX[k], sibling)

        for j in range(8 + LATE):
            each(lambda: zero(j), lambda: one(j))
            yield
        for i in range(8):
            got(buf.at[:, zat(AG_ORDER[i]), 1 - core, :, lo:hi], rr.at[36 + i])
        yield

    def halves(lo, hi, stage, group):
        ss, rr = ring_s.at[stage], ring_r.at[stage]
        for i in group:
            zz = zat(RS_ORDER[i])
            one = rcopy(part.at[:, zz, 1 - core, :, lo:hi], sib.at[:, zz, :, lo:hi], ss.at[44 + i], rr.at[36 + i], sibling)
            one.start()
            done.append(one)

    def total_of(terms):
        total = terms[0][...].astype(F32)
        for term in terms[1:]:
            total = total + term[...].astype(F32)
        return total

    def scatter(lo, hi, stage):
        ss, rr = ring_s.at[stage], ring_r.at[stage]
        count = [0, 0]

        def slot(r):
            return recv.at[r, :, lo:hi]

        def send(c, src, r, device):
            rcopy(src, slot(r), ss.at[count[c]], rr.at[r], device).start()
            sent[c].append((lambda: slot(0), ring_s, (stage, count[c])))
            count[c] += 1

        def mine(c, xx, s):
            return part.at[xx, zat(s), c, :, lo:hi]

        def theirs(xx, s):
            return sib.at[xx, zat(s), :, lo:hi]

        def add(dst, terms):
            dst[...] = total_of(terms).astype(BF16)

        def finish(c, terms):
            errs[x, z, c, :, lo:hi] = (total_of(terms) - tgt[:, lo:hi]).astype(BF16)

        def across(i):
            s = RS_ORDER[i]
            got(sib.at[:, zat(s), :, lo:hi], rr.at[36 + i])
            for d in (2, 1, 3):
                add(mine(0, xat(d), s), [mine(0, xat(d), s), theirs(xat(d), s)])
                send(0, mine(0, xat(d), s), 8 * (d - 1) + i, xd(d))

        passes = {4: (-2, 26, ()), 3: (1, 24, ()), -3: (-1, 25, ()), 2: (2, 29, (24,)), -2: (-2, 30, (25, 26)),
                  1: (1, 27, ()), -1: (-1, 28, ()), 0: (0, 0, (27, 28, 29, 30))}

        def along(i):
            s = RS_ORDER[i]
            terms = [mine(0, x, s), theirs(x, s)]
            to, there, before = passes[s]
            for r in (i, 8 + i, 16 + i) + before:
                got(slot(r), rr.at[r])
                terms.append(slot(r))
            if s == 0:
                finish(0, terms)
            else:
                add(mine(0, x, s), terms)
                send(0, mine(0, x, s), there, zd(to))

        def zero(j):
            if j < 8:
                across(j)
            if LATE <= j < LATE + 8:
                along(j - LATE)

        def one(j):
            if j < 8:
                s = RS_ORDER[j]
                k = abs(s)
                got(sib.at[:, zat(s), :, lo:hi], rr.at[36 + j])
                for d in (2, 1, 3, 0):
                    xx = xat(d)
                    terms = [mine(1, xx, s), theirs(xx, s)]
                    for here, base in ((0 <= s < 4 and (k < 3 or d < 2), 0), (-4 < s <= 0 and (k < 3 or d >= 2), 16)):
                        if here:
                            got(slot(base + 4 * k + d), rr.at[base + 4 * k + d])
                            terms.append(slot(base + 4 * k + d))
                    add(mine(1, xx, s), terms)
                    if s == 4:
                        send(1, mine(1, xx, s), (0 if d < 2 else 16) + 12 + d, zd(1) if d < 2 else zd(-1))
                    elif s > 0:
                        send(1, mine(1, xx, s), 4 * (k - 1) + d, zd(1))
                    elif s < 0:
                        send(1, mine(1, xx, s), 16 + 4 * (k - 1) + d, zd(-1))
                    elif d:
                        send(1, mine(1, xx, s), 32 + d, xd(d))
            elif j == 7 + LATE:
                terms = [mine(1, x, 0)]
                for d in (1, 2, 3):
                    got(slot(32 + d), rr.at[32 + d])
                    terms.append(slot(32 + d))
                finish(1, terms)

        for j in range(8 + LATE):
            each(lambda: zero(j), lambda: one(j))
            yield

    def pieces(buf, layer, zs):
        lo = BASE[layer]
        rows = 768 if zs == slice(0, 8) else 384
        for xx in range(4):
            yield buf[xx, zs, :, :, lo:lo + MAIN].reshape(rows, MAIN), MAIN * xx
        rest = [buf[2 * layer + j, zs, :, :, MAIN:MAIN + REST].reshape(rows, REST) for j in range(2)]
        yield jnp.concatenate(rest, axis=1), 4 * MAIN

    bias = jnp.where(xhi == 0, eb[:, :FH], eb[:, FH:])

    def encode(s, half):
        rows = slice(384 * half, 384 * half + 384)
        zs = slice(4 * half, 4 * half + 4)
        value = bias[s:s + 1]
        for cols, first in pieces(acts, s, zs):
            value = value + jnp.dot(cols, ew[s, first:first + cols.shape[1]], preferred_element_type=F32)
        active = jnp.maximum(value, 0.0)
        gate[s, rows] = active
        code = (0.5 * active * active).astype(BF16)
        coded[s, zs] = code.reshape(4, 96, FH)
        coded_t[s, :, rows] = code.T

    def decode(t, xx, group):
        width = MAIN if xx < 4 else 2 * REST
        total = None
        for s in range(t + 1):
            codes = jnp.concatenate([coded[s, zat(RS_ORDER[i])] for i in group], axis=0)
            term = jnp.dot(codes, dw[PAIR[s, t], :, MAIN * xx:MAIN * xx + width], preferred_element_type=F32)
            total = term if total is None else total + term
        total = total.astype(BF16)
        for n, i in enumerate(group):
            rows = total[96 * n:96 * n + 96]
            zz = zat(RS_ORDER[i])
            if xx < 4:
                part[xx, zz, :, :, BASE[t]:BASE[t] + MAIN] = rows.reshape(2, ROWS, MAIN)
            else:
                for j in range(2):
                    part[2 * t + j, zz, :, :, MAIN:MAIN + REST] = rows[:, REST * j:REST * j + REST].reshape(2, ROWS, REST)

    def start(src, dst, n, d):
        one = rcopy(src, dst, y_s.at[n], y_r.at[n], yd(d))
        one.start()
        done.append(one)

    def first(n, block, one):
        start(block.at[(y + 2) % YN, 0], one.at[0], 4 * n, 1)
        start(block.at[(y + 2) % YN, 1], one.at[1], 4 * n + 1, 3)

    def accumulate(dst, terms, rows):
        def some(r, carry):
            sl = pl.ds(pl.multiple_of(r * 32, 32), 32)
            total = terms[0][sl, :].astype(F32)
            for term in terms[1:]:
                total = total + term[sl, :].astype(F32)
            dst[sl, :] = total.astype(BF16)
            return carry

        lax.fori_loop(0, rows // 32, some, 0)

    def second(n, block, one, two, rows):
        for j, d in ((0, 1), (1, 3)):
            got(one.at[j], y_r.at[4 * n + j])
            mine = block.at[(y + d) % YN, j]
            accumulate(mine, [mine, one.at[j]], rows)
            start(block.at[(y + d) % YN], two.at[j], 4 * n + 2 + j, d)

    def last(n, two):
        for j in range(2):
            got(two.at[j], y_r.at[4 * n + 2 + j])

    whole = slice(0, 8)

    def dec_grad(s, t):
        p = PAIR[s, t]
        for cols, at in pieces(errs, t, whole):
            width = cols.shape[1]
            value = jnp.dot(coded_t[s], cols, preferred_element_type=F32) * scale
            gdec[p, :, :, :, at:at + width] = value.astype(BF16).reshape(YN, 2, 32, width)
        first(p, gdec.at[p], rone_d.at[p])

    def dcoded(s):
        total_bias = jnp.zeros((1, FH), F32)
        for half in range(2):
            rows = slice(384 * half, 384 * half + 384)
            value = None
            for t in range(s, 2):
                for cols, at in pieces(errs, t, slice(4 * half, 4 * half + 4)):
                    term = lax.dot_general(cols, dw[PAIR[s, t], :, at:at + cols.shape[1]],
                                           (((1,), (1,)), ((), ())), preferred_element_type=F32)
                    value = term if value is None else value + term
            grad = (value * gate[s, rows]).astype(BF16)
            dpre[s, rows] = grad
            total_bias = total_bias + jnp.sum(grad.astype(F32), axis=0, keepdims=True)
        bsum[s:s + 1, :] = total_bias * scale

    def enc_grad(s):
        for cols, at in pieces(acts, s, whole):
            value = lax.dot_general(cols, dpre[s], (((0,), (0,)), ((), ())), preferred_element_type=F32) * scale
            value = value.astype(BF16)
            row, end = at, at + cols.shape[1]
            while row < end:
                stop = min(end, (row // 288 + 1) * 288)
                owner, place_ = row // 288, row % 288
                genc[s, owner % YN, owner // YN, place_:place_ + stop - row] = value[row - at:stop - at]
                row = stop
        first(3 + s, genc.at[s], rone_e.at[s])

    def dec_second(p):
        second(p, gdec.at[p], rone_d.at[p], rtwo_d.at[p], 32)

    def enc_second(s):
        second(3 + s, genc.at[s], rone_e.at[s], rtwo_e.at[s], 288)

    def dec_out(p):
        last(p, rtwo_d.at[p])
        for j in range(2):
            accumulate(gd_out.at[p, 32 * j:32 * j + 32], [gdec.at[p, y, j], rtwo_d.at[p, 0, j], rtwo_d.at[p, 1, j]], 32)

    def enc_out(s):
        last(3 + s, rtwo_e.at[s])
        for j in range(2):
            mine = genc.at[s, y, j]
            accumulate(mine, [mine, rtwo_e.at[s, 0, j], rtwo_e.at[s, 1, j]], 288)
        one = rcopy(genc.at[s, y, 1 - xhi], swap.at[s], sw_s.at[s], sw_r.at[s], xd(2))
        one.start()
        done.append(one)

    def turn(*steps):
        more = [next(one, "end") is None for one in steps]
        return more[0]

    inputs = gather(acts, 0, COLS, 0)
    while turn(inputs):
        pass
    for copy in w_copies:
        copy.wait()
    for s in range(2):
        for half in range(2):
            encode(s, half)
    one, zero = (MAIN, COLS), (0, MAIN)
    for group in (range(4), range(4, 8)):
        for xx in range(5):
            decode(1, xx, group)
        decode(0, 4, group)
        halves(*one, 1, group)
    for group in (range(4), range(4, 8)):
        for xx in range(4):
            decode(0, xx, group)
        halves(*zero, 2, group)
    early = scatter(*one, 1)
    while turn(early):
        pass
    early, late = gather(errs, *one, 3), scatter(*zero, 2)
    while turn(early, late):
        pass
    while turn(late):
        pass
    later = gather(errs, *zero, 4)
    turn(later)
    dec_grad(0, 1)
    turn(later)
    dec_grad(1, 1)
    turn(later)
    dec_second(1)
    turn(later)
    dec_second(2)
    turn(later)
    dcoded(1)
    turn(later)
    enc_grad(1)
    turn(later)
    turn(later)
    turn(later)
    enc_second(1)
    while turn(later):
        pass
    dcoded(0)
    enc_grad(0)
    dec_grad(0, 0)
    for d in (1, 2, 3):
        one = rcopy(bsum, bland.at[d], b_s.at[d], b_r.at[d], yd(d))
        one.start()
        done.append(one)
    enc_second(0)
    dec_second(0)
    dec_out(1)
    dec_out(2)
    enc_out(1)
    enc_out(0)
    for d in (1, 2, 3):
        got(bland.at[d], b_r.at[d])
    total = bsum[...] + bland[1] + bland[2] + bland[3]
    own = jnp.where(y == 0, total[:, :64], 0.0)
    for n in range(1, YN):
        own = own + jnp.where(y == n, total[:, 64 * n:64 * n + 64], 0.0)
    gb_out[...] = own[:2]
    dec_out(0)
    for s in (1, 0):
        got(swap.at[s], sw_r.at[s])

        @pl.when(xhi == 0)
        def _():
            ge_out[s, :, :FH] = genc[s, y, 0]
            ge_out[s, :, FH:] = swap[s]

        @pl.when(xhi == 1)
        def _():
            ge_out[s, :, :FH] = swap[s]
            ge_out[s, :, FH:] = genc[s, y, 1]

    for one in sends + done:
        one.wait_send()

    def drain(c):
        for like, sems, at in sent[c]:
            rcopy(like(), like(), sems.at[at], sems.at[at], sibling).wait_send()

    each(lambda: drain(0), lambda: drain(1))


def shards(acts_in, targets, enc_weight, enc_bias, dec_weight):
    both = jnp.stack([acts_in, targets])
    main = both[..., :4 * MAIN].reshape(2, TD, 2, 4, MAIN)
    rest = both[..., 4 * MAIN:].reshape(2, TD, 4, REST)
    both = jnp.concatenate([main[:, :, 0], rest, main[:, :, 1]], axis=-1).transpose(0, 2, 1, 3)
    both = jnp.pad(both, ((0, 0), (0, 0), (0, 16 - TD), (0, 0)))
    dma = pltpu.SemaphoreType.DMA
    unit = (ROWS, COLS)
    vmem = pl.BlockSpec(memory_space=pltpu.VMEM)
    hbm = pl.BlockSpec(memory_space=pl.ANY)
    ge, gb, gd = pl.pallas_call(
        kernel,
        out_shape=(
            jax.ShapeDtypeStruct((2, 288, 512), BF16),
            jax.ShapeDtypeStruct((2, 64), F32),
            jax.ShapeDtypeStruct((3, 64, 2304), BF16),
        ),
        in_specs=[vmem, vmem, hbm, hbm],
        out_specs=(vmem, vmem, vmem),
        scratch_shapes=[
            pltpu.VMEM((2, XN, 16, COLS), BF16),
            pltpu.VMEM((XN, ZN, 2) + unit, BF16),
            pltpu.VMEM(unit, F32),
            pltpu.VMEM((XN, ZN, 2) + unit, BF16),
            pltpu.VMEM((2, 2304, FH), BF16),
            pltpu.VMEM((3, FH, 2304), BF16),
            pltpu.VMEM((2, 768, FH), F32),
            pltpu.VMEM((2, ZN, 96, FH), BF16),
            pltpu.VMEM((2, FH, 768), BF16),
            pltpu.VMEM((2, 768, FH), BF16),
            pltpu.VMEM((XN, ZN, 2) + unit, BF16),
            pltpu.VMEM((XN, ZN) + unit, BF16),
            pltpu.VMEM((36,) + unit, BF16),
            pltpu.VMEM((3, YN, 2, 32, 2304), BF16),
            pltpu.VMEM((2, YN, 2, 288, FH), BF16),
            pltpu.VMEM((3, 2, 32, 2304), BF16),
            pltpu.VMEM((2, 2, 288, FH), BF16),
            pltpu.VMEM((3, 2, 2, 32, 2304), BF16),
            pltpu.VMEM((2, 2, 2, 288, FH), BF16),
            pltpu.VMEM((2, 288, FH), BF16),
            pltpu.VMEM((8, FH), F32),
            pltpu.VMEM((4, 8, FH), F32),
            dma((2,)), dma((4,)), dma((4,)),
            dma((5, 52)), dma((5, 44)),
            dma((20,)), dma((20,)), dma((4,)), dma((4,)), dma((2,)), dma((2,)),
        ],
        compiler_params=pltpu.CompilerParams(collective_id=0, has_side_effects=True, vmem_limit_bytes=67_000_000),
    )(both, enc_bias, enc_weight, dec_weight)
    return ge, gb, gd


def solution(mesh):
    return jax.shard_map(
        shards,
        mesh=mesh,
        in_specs=(
            P(("tok", "feat"), None, None),
            P(("tok", "feat"), None, None),
            P(None, None, "feat"),
            P(None, "feat"),
            P(None, "feat", None),
        ),
        out_specs=(
            P(None, "tok", "feat"),
            P(None, ("feat", "tok")),
            P(None, ("feat", "tok"), None),
        ),
        check_vma=False,
    )
```
